32 devices in a mesh: rows: 8 (over y, x, core), cols: 4 (over z).
Axes of the slice: x: 2, y: 2, z: 4, core: 2. Of those that a mesh axis runs over, the one named last changes fastest.
Arguments:
- block_values: bfloat16 [16384, 128], P(('rows', 'cols')), may hold values from -6 to 6
- block_length: int32 [16384], P(('rows', 'cols')), may hold values from 1 to 128
- block_owner: int32 [16384], P(('rows', 'cols')), may hold values from 0 to 4095, as said below
- block_second: int32 [16384], P(('rows', 'cols')), may hold values from 0 to 4095, as said below
- block_third: int32 [16384, 128], P(('rows', 'cols')), may hold values from 0 to 8191
- live_blocks: int32 [32], P(('rows', 'cols')), may hold values from 1 to 512, as said below
- second_factor: bfloat16 [4096, 256], P('cols', 'rows')
- third_factor: bfloat16 [8192, 256], P('cols', 'rows'), may hold values from -6 to 6
Outputs:
- first_factor: float32 [4096, 256], P('cols', 'rows')
The draws below stay inside these ranges and needn't reach their ends.
Inputs may be any that keep to these rules, and one draw needn't show every extreme that they name: `block_owner`: slot b lies on device d = b // 512 with index r along rows; its row lies in r * 4096 // 8 up to (r + 1) * 4096 // 8 - 1, the device's mode-1 slab. `block_second`: slot b lies on device d = b // 512 with index c along cols; its row lies in c * 4096 // 4 up to (c + 1) * 4096 // 4 - 1. `live_blocks`: some device uses all 512 slots in every draw.
All inputs are finite; a program needn't handle non-finite values.
Results may differ from the reference program's by a relative error of at most 0.0003.
Values may be sent and summed in bfloat16 or wider, within the bound.
A program may use at most 128 MiB of HBM per device.

```python
import jax
import jax.numpy as jnp
from jax import lax

R = 256
L = 128
NB_DEV = 512
BLOCKS = 16384
I = 4096
J = 4096
K = 8192
N_ROWS = 8
N_COLS = 4
DEVICES = 32


def draw_block_owner(key, part):
    slot = jnp.arange(NB_DEV * DEVICES, dtype=jnp.int32)
    device = slot // NB_DEV
    slab = I // N_ROWS
    offset = jax.random.randint(key, (NB_DEV * DEVICES,), 0, slab, dtype=jnp.int32)
    return device // N_COLS * slab + offset


def draw_block_second(key, part):
    slot = jnp.arange(NB_DEV * DEVICES, dtype=jnp.int32)
    device = slot // NB_DEV
    span = J // N_COLS
    offset = jax.random.randint(jax.random.fold_in(key, 7), (NB_DEV * DEVICES,), 0, span, dtype=jnp.int32)
    return device % N_COLS * span + offset


def draw_live_blocks(key, part):
    first, second = jax.random.split(jax.random.fold_in(key, 11))
    counts = jax.random.randint(first, (DEVICES,), 1, NB_DEV + 1, dtype=jnp.int32)
    full = jax.random.randint(second, (), 0, DEVICES, dtype=jnp.int32)
    return jnp.where(jnp.arange(DEVICES, dtype=jnp.int32) == full, NB_DEV, counts)


def draw_second_factor(key, part):
    first = jax.random.fold_in(jax.random.fold_in(key, 13), 0)
    third = jax.random.fold_in(jax.random.fold_in(key, 13), 2)
    trend = 3.0 ** (jnp.arange(J, dtype=jnp.float32) / J)
    scale = trend * 10.0 ** jax.random.uniform(first, (J,), jnp.float32)
    base = jax.random.normal(third, (J, R), jnp.float32)
    return (scale[:, None] * base).astype(jnp.bfloat16)


def place_ends(drawn, stream_key, low, top_value):
    longest = drawn.shape.index(max(drawn.shape))
    spots = []
    for shift in (0, 1):
        where = [jax.random.randint(jax.random.fold_in(stream_key, axis), (), 0, length) for axis, length in enumerate(drawn.shape)]
        where[longest] = (where[longest] + shift) % drawn.shape[longest]
        spots.append(tuple(where))
    return drawn.at[spots[0]].set(low).at[spots[1]].set(top_value)


def steps_of(key, dims, cuts, smallest, high):
    gain = 1.0
    for dim, blocks in cuts:
        draws = jax.random.uniform(jax.random.fold_in(jax.random.fold_in(key, 6), dim), (blocks,), jnp.float32, smallest / len(cuts), high / len(cuts))
        gain = gain * jnp.repeat(jnp.exp(draws), dims[dim] // blocks).reshape((-1,) + (1,) * (len(dims) - 1 - dim))
    return gain


def scatter_about(own_key, dims, deviation, reach, shards=(), kind=jnp.bfloat16):
    values = jax.random.normal(own_key, dims, jnp.float32) * deviation
    if len(shards) > 0:
        values = steps_of(own_key, dims, shards, -0.22, 0.18) * values
    return jnp.clip(values, min=-reach, max=reach).astype(kind)


def setup_inputs(seed: int = 0) -> dict:
    key_of = jax.random.split(jax.random.key(seed), 9)
    return {
        "block_values": scatter_about(key_of[0], (BLOCKS, L), 1.0, 6.0, ((0, 32),)),
        "block_length": place_ends(jax.random.randint(key_of[1], (BLOCKS,), 1, L + 1), jax.random.fold_in(key_of[1], 1), 1, L).astype(jnp.int32),
        "block_owner": draw_block_owner(jax.random.fold_in(key_of[8], 71), 0),
        "block_second": draw_block_second(jax.random.fold_in(key_of[8], 71), 0),
        "block_third": place_ends(jax.random.randint(key_of[4], (BLOCKS, L), 0, K), jax.random.fold_in(key_of[4], 1), 0, K - 1).astype(jnp.int32),
        "live_blocks": draw_live_blocks(jax.random.fold_in(key_of[8], 71), 0),
        "second_factor": draw_second_factor(jax.random.fold_in(key_of[8], 71), 0),
        "third_factor": scatter_about(key_of[7], (K, R), 1.0, 6.0, ((0, 4), (1, 8))),
    }


def reference(block_values, block_length, block_owner, block_second, block_third, live_blocks, second_factor, third_factor):
    nblk = block_values.shape[0]
    width = block_values.shape[1]
    group = min(nblk, 512)
    position = jnp.arange(nblk, dtype=jnp.int32)
    live_block = position % NB_DEV < live_blocks[position // NB_DEV]
    lane = jnp.arange(width, dtype=jnp.int32)
    live = (lane[None, :] < block_length[:, None]) & live_block[:, None]
    masked = jnp.where(live, block_values, jnp.zeros((), jnp.bfloat16))
    steps = nblk // group

    def accumulate(total, pieces):
        values, third, second, owner = pieces
        rows = third_factor[third].astype(jnp.float32)
        fold = jnp.einsum('gt,gtr->gr', values.astype(jnp.float32), rows)
        contrib = second_factor[second].astype(jnp.float32) * fold
        return (total.at[owner].add(contrib), None)
    pieces = (masked.reshape(steps, group, width), block_third.reshape(steps, group, width), block_second.reshape(steps, group), block_owner.reshape(steps, group))
    start = jnp.zeros((I, R), jnp.float32)
    mttkrp, unused = lax.scan(accumulate, start, pieces)
    contract = (((0,), (0,)), ((), ()))
    gram_second = lax.dot_general(second_factor.astype(jnp.float32), second_factor.astype(jnp.float32), contract, preferred_element_type=jnp.float32) / J
    gram_third = lax.dot_general(third_factor.astype(jnp.float32), third_factor.astype(jnp.float32), contract, preferred_element_type=jnp.float32) / K
    gram = gram_second * gram_third
    factor = jnp.linalg.cholesky(gram)
    return jax.scipy.linalg.cho_solve((factor, True), mttkrp.T).T
```

```python
import functools

import jax
import jax.numpy as jnp
from jax import lax
from jax.experimental import pallas as pl
from jax.experimental.pallas import tpu as pltpu
from jax.sharding import PartitionSpec as P

LO = 256
BF = jnp.bfloat16
F32 = jnp.float32
NT = (((1,), (1,)), ((), ()))
NN = (((1,), (0,)), ((), ()))
TN = (((0,), (0,)), ((), ()))


def dot(a, b, dims, precision=None):
    return lax.dot_general(a, b, dims, precision=precision, preferred_element_type=F32)


def spread_kernel(group, n_hi, count_ref, values_ref, length_ref, third_ref, high_ref, low_ref, masked, rows):
    width = values_ref.shape[1]
    base = pl.program_id(0) * group
    lane = lax.broadcasted_iota(jnp.int32, (group, width), 1)
    slot = lax.broadcasted_iota(jnp.int32, (group, width), 0) + base
    live = (lane < length_ref[...]) & (slot < count_ref[0])
    masked[...] = jnp.where(live, values_ref[...].astype(F32), 0.0)
    at_hi = lax.broadcasted_iota(jnp.int32, (n_hi, width), 0)
    at_lo = lax.broadcasted_iota(jnp.int32, (LO, width), 0)

    def eight(step, carry):
        first = pl.multiple_of(step * 8, 8)
        index = third_ref[pl.ds(first, 8), :]
        value = masked[pl.ds(first, 8), :]
        index_hi = index // LO
        index_lo = index - index_hi * LO
        for j in range(8):
            left = jnp.where(at_hi == index_hi[j : j + 1, :], value[j : j + 1, :], 0.0).astype(BF)
            right = jnp.where(at_lo == index_lo[j : j + 1, :], 1.0, 0.0).astype(BF)
            dense = dot(left, right, NT)
            start = pl.multiple_of((first + j) * n_hi, n_hi)
            for piece in range(LO // 128):
                rows[piece, pl.ds(start, n_hi), :] = dense[:, piece * 128 : (piece + 1) * 128]
        return carry

    lax.fori_loop(0, group // 8, eight, 0)
    for h in range(n_hi):
        for piece in range(LO // 128):
            part = rows[piece, pl.ds(h, group, stride=n_hi), :]
            high = part.astype(BF)
            high_ref[h, :, piece * 128 : (piece + 1) * 128] = high
            low_ref[h, :, piece * 128 : (piece + 1) * 128] = (part - high.astype(F32)).astype(BF)


def spread(count, values, length, third, n_hi):
    nblk, width = values.shape
    group = min(nblk, 64)
    return pl.pallas_call(
        functools.partial(spread_kernel, group, n_hi),
        grid=(nblk // group,),
        in_specs=[
            pl.BlockSpec(memory_space=pltpu.SMEM),
            pl.BlockSpec((group, width), lambda g: (g, 0)),
            pl.BlockSpec((group, 1), lambda g: (g, 0)),
            pl.BlockSpec((group, width), lambda g: (g, 0)),
        ],
        out_specs=[pl.BlockSpec((n_hi, group, LO), lambda g: (0, g, 0))] * 2,
        out_shape=[jax.ShapeDtypeStruct((n_hi, nblk, LO), BF)] * 2,
        scratch_shapes=[pltpu.VMEM((group, width), F32), pltpu.VMEM((LO // 128, group * n_hi, 128), F32)],
        compiler_params=pltpu.CompilerParams(vmem_limit_bytes=40 * 1024 * 1024),
        cost_estimate=pl.CostEstimate(flops=20_000_000_000, bytes_accessed=4 * n_hi * nblk * LO, transcendentals=0),
        name="spread",
    )(count, values, length, third)


def fold_kernel(per, high_ref, low_ref, third_ref, second_ref, pick_ref, owner_ref, out_ref, fold):
    step = pl.program_id(0)
    nblk = fold.shape[0]

    @pl.when(step == 0)
    def _():
        fold[...] = jnp.zeros_like(fold)

    total = None
    for h in range(per):
        table = third_ref[h * LO : (h + 1) * LO, :]
        term = dot(high_ref[h], table, NN) + dot(low_ref[h], table, NN)
        total = term if total is None else total + term
    fold[...] += total

    @pl.when(step == pl.num_programs(0) - 1)
    def _():
        at = lax.broadcasted_iota(jnp.int32, (nblk, second_ref.shape[0]), 1)
        pick = jnp.where(at == pick_ref[...], 1.0, 0.0).astype(BF)
        contrib = dot(pick, second_ref[...], NN) * fold[...]
        at = lax.broadcasted_iota(jnp.int32, (out_ref.shape[0], nblk), 0)
        place = jnp.where(at == owner_ref[...], 1.0, 0.0).astype(BF)
        high = contrib.astype(BF)
        rest = contrib - high.astype(F32)
        middle = rest.astype(BF)
        low = (rest - middle.astype(F32)).astype(BF)
        out_ref[...] = dot(place, high, NN) + (dot(place, middle, NN) + dot(place, low, NN))


def fold_rows(high, low, third, second, pick, owner, slab):
    n_hi, nblk, lo = high.shape
    rank = third.shape[1]
    per = min(n_hi, 4)
    return pl.pallas_call(
        functools.partial(fold_kernel, per),
        grid=(n_hi // per,),
        in_specs=[
            pl.BlockSpec((per, nblk, lo), lambda g: (g, 0, 0)),
            pl.BlockSpec((per, nblk, lo), lambda g: (g, 0, 0)),
            pl.BlockSpec((per * lo, rank), lambda g: (g, 0)),
            pl.BlockSpec(second.shape, lambda g: (0, 0)),
            pl.BlockSpec((nblk, 1), lambda g: (0, 0)),
            pl.BlockSpec((1, nblk), lambda g: (0, 0)),
        ],
        out_specs=pl.BlockSpec((slab, rank), lambda g: (0, 0)),
        out_shape=jax.ShapeDtypeStruct((slab, rank), F32),
        scratch_shapes=[pltpu.VMEM((nblk, rank), F32)],
        compiler_params=pltpu.CompilerParams(vmem_limit_bytes=50 * 1024 * 1024),
        cost_estimate=pl.CostEstimate(flops=10_000_000_000, bytes_accessed=4 * n_hi * nblk * lo, transcendentals=0),
        name="fold_rows",
    )(high, low, third, second, pick, owner)


def small_inverse(block):
    n = block.shape[0]
    down = lax.broadcasted_iota(jnp.int32, (n, n), 0)
    across = lax.broadcasted_iota(jnp.int32, (n, n), 1)
    for j in range(n):
        column = block[:, j : j + 1]
        pivot = 1.0 / block[j : j + 1, j : j + 1]
        cleared = jnp.where(across == j, jnp.where(down == j, 1.0, 0.0), block)
        row = cleared[j : j + 1, :] * pivot
        block = jnp.where(down == j, row, cleared - column * row)
    return block


def invert_kernel(size, gram_ref, out_ref):
    rank = gram_ref.shape[1]
    exact = lax.Precision.HIGHEST
    a = gram_ref[0] * gram_ref[1]
    down = lax.broadcasted_iota(jnp.int32, (rank, size), 0)
    eye = jnp.where(
        lax.broadcasted_iota(jnp.int32, (size, size), 0) == lax.broadcasted_iota(jnp.int32, (size, size), 1), 1.0, 0.0
    )
    for k in range(rank // size):
        s, e = k * size, (k + 1) * size
        inverse = small_inverse(a[s:e, s:e])
        column = jnp.where((down >= s) & (down < e), 0.0, a[:, s:e])
        pieces = [a[s:e, :s]] * (s > 0) + [eye] + [a[s:e, e:]] * (e < rank)
        row = dot(inverse, jnp.concatenate(pieces, axis=1), NN, exact)
        zero = jnp.zeros((rank, size), F32)
        pieces = [a[:, :s]] * (s > 0) + [zero] + [a[:, e:]] * (e < rank)
        a = jnp.concatenate(pieces, axis=1) - dot(column, row, NN, exact)
        pieces = [a[:s]] * (s > 0) + [row] + [a[e:]] * (e < rank)
        a = jnp.concatenate(pieces, axis=0)
    out_ref[...] = a


def invert(grams):
    rank = grams.shape[1]
    return pl.pallas_call(
        functools.partial(invert_kernel, 32),
        out_shape=jax.ShapeDtypeStruct((rank, rank), F32),
        cost_estimate=pl.CostEstimate(flops=10_000_000_000, bytes_accessed=1_000_000, transcendentals=0),
        name="invert",
    )(grams)


def per_device(
    block_values,
    block_length,
    block_owner,
    block_second,
    block_third,
    live_blocks,
    second_factor,
    third_factor,
):
    n_rows = lax.axis_size("rows")
    n_cols = lax.axis_size("cols")
    row_at = lax.axis_index("rows")
    col_at = lax.axis_index("cols")
    nblk = block_values.shape[0]
    range_rows = second_factor.shape[0]
    third_rows = third_factor.shape[0]
    whole_third = third_rows * n_cols
    slab = range_rows * n_cols // n_rows

    both = lax.all_gather(jnp.concatenate([third_factor, second_factor], axis=0), "rows", axis=1, tiled=True)
    third_range = both[:third_rows]
    second_range = both[third_rows:]
    third_whole = lax.all_gather(third_range, "cols", axis=0, tiled=True)
    grams = jnp.stack(
        [
            dot(second_range, second_range, TN) / (range_rows * n_cols),
            dot(third_range, third_range, TN) / whole_third,
        ]
    )
    inverse = invert(lax.psum(grams, "cols"))

    high, low = spread(live_blocks, block_values, block_length[:, None], block_third, whole_third // LO)
    partial_rows = fold_rows(
        high,
        low,
        third_whole,
        second_range,
        (block_second - col_at * range_rows)[:, None],
        (block_owner - row_at * slab)[None, :],
        slab,
    )
    mine = lax.psum_scatter(partial_rows, "cols", scatter_dimension=0, tiled=True)
    solved = dot(mine, inverse, NN, lax.Precision.HIGHEST)
    moved = lax.all_to_all(
        lax.all_to_all(solved, "rows", split_axis=1, concat_axis=0, tiled=True),
        "cols",
        split_axis=0,
        concat_axis=0,
        tiled=True,
    )
    share = n_rows // n_cols
    owned_rows = mine.shape[0]
    reordered = moved.reshape(n_cols, share, owned_rows, moved.shape[1]).transpose(1, 0, 2, 3)
    return reordered.reshape(n_rows * owned_rows, moved.shape[1])


def solution(mesh):
    return jax.shard_map(
        per_device,
        mesh=mesh,
        in_specs=(
            P(("rows", "cols"), None),
            P(("rows", "cols")),
            P(("rows", "cols")),
            P(("rows", "cols")),
            P(("rows", "cols"), None),
            P(("rows", "cols")),
            P("cols", "rows"),
            P("cols", "rows"),
        ),
        out_specs=P("cols", "rows"),
        check_vma=False,
    )
```

```python
import functools

import jax
import jax.numpy as jnp
from jax import lax
from jax.experimental import pallas as pl
from jax.experimental.pallas import tpu as pltpu
from jax.sharding import PartitionSpec as P

LO = 256
BF = jnp.bfloat16
F32 = jnp.float32
NT = (((1,), (1,)), ((), ()))
NN = (((1,), (0,)), ((), ()))
TN = (((0,), (0,)), ((), ()))


def dot(a, b, dims, precision=None):
    return lax.dot_general(a, b, dims, precision=precision, preferred_element_type=F32)


def spread_kernel(group, n_hi, first_slot, count_ref, turn_ref, values_ref, length_ref, third_ref, high_ref, low_ref, masked, rows):
    width = values_ref.shape[1]
    base = pl.program_id(0) * group + first_slot
    turn = turn_ref[0]
    lane = lax.broadcasted_iota(jnp.int32, (group, width), 1)
    slot = lax.broadcasted_iota(jnp.int32, (group, width), 0) + base
    live = (lane < length_ref[...]) & (slot < count_ref[0])
    masked[...] = jnp.where(live, values_ref[...].astype(F32), 0.0)
    at_hi = lax.broadcasted_iota(jnp.int32, (n_hi, width), 0)
    at_lo = lax.broadcasted_iota(jnp.int32, (LO, width), 0)

    def eight(step, carry):
        first = pl.multiple_of(step * 8, 8)
        index = third_ref[pl.ds(first, 8), :] - turn
        index = jnp.where(index < 0, index + n_hi * LO, index)
        value = masked[pl.ds(first, 8), :]
        index_hi = index // LO
        index_lo = index - index_hi * LO
        for j in range(8):
            left = jnp.where(at_hi == index_hi[j : j + 1, :], value[j : j + 1, :], 0.0).astype(BF)
            right = jnp.where(at_lo == index_lo[j : j + 1, :], 1.0, 0.0).astype(BF)
            dense = dot(left, right, NT)
            start = pl.multiple_of((first + j) * n_hi, n_hi)
            for piece in range(LO // 128):
                rows[piece, pl.ds(start, n_hi), :] = dense[:, piece * 128 : (piece + 1) * 128]
        return carry

    lax.fori_loop(0, group // 8, eight, 0)
    for h in range(n_hi):
        for piece in range(LO // 128):
            part = rows[piece, pl.ds(h, group, stride=n_hi), :]
            high = part.astype(BF)
            high_ref[h, :, piece * 128 : (piece + 1) * 128] = high
            low_ref[h, :, piece * 128 : (piece + 1) * 128] = (part - high.astype(F32)).astype(BF)


def spread(count, turn, values, length, third, n_hi, start, stop):
    nblk = stop - start
    width = values.shape[1]
    group = min(nblk, 64)
    skip = start // group
    return pl.pallas_call(
        functools.partial(spread_kernel, group, n_hi, start),
        grid=(nblk // group,),
        in_specs=[
            pl.BlockSpec(memory_space=pltpu.SMEM),
            pl.BlockSpec(memory_space=pltpu.SMEM),
            pl.BlockSpec((group, width), lambda g: (g + skip, 0)),
            pl.BlockSpec((group, 1), lambda g: (g + skip, 0)),
            pl.BlockSpec((group, width), lambda g: (g + skip, 0)),
        ],
        out_specs=[pl.BlockSpec((n_hi, group, LO), lambda g: (0, g, 0))] * 2,
        out_shape=[jax.ShapeDtypeStruct((n_hi, nblk, LO), BF)] * 2,
        scratch_shapes=[pltpu.VMEM((group, width), F32), pltpu.VMEM((LO // 128, group * n_hi, 128), F32)],
        compiler_params=pltpu.CompilerParams(vmem_limit_bytes=40 * 1024 * 1024),
        cost_estimate=pl.CostEstimate(flops=40_000_000 * nblk, bytes_accessed=4 * n_hi * nblk * LO, transcendentals=0),
        name="spread",
    )(count, turn, values, length, third)


def fold_kernel(per, cuts, *refs):
    n = len(cuts)
    highs, lows = refs[:n], refs[n : 2 * n]
    mine_ref, other_ref, second_mine_ref, second_other_ref, pick_ref, owner_ref, out_ref, gram_ref, fold = refs[2 * n :]
    step = pl.program_id(0)
    nblk = fold.shape[0]

    @pl.when(step == 0)
    def _():
        fold[...] = jnp.zeros_like(fold)
        gram_ref[...] = jnp.zeros_like(gram_ref)

    table = jnp.concatenate([mine_ref[...], other_ref[...]], axis=0)
    gram_ref[...] += dot(table, table, NT)
    for i, (start, stop) in enumerate(cuts):
        total = fold[start:stop, :]
        for h in range(per):
            piece = table[:, h * LO : (h + 1) * LO]
            total = total + (dot(highs[i][h], piece, NT) + dot(lows[i][h], piece, NT))
        fold[start:stop, :] = total

    @pl.when(step == pl.num_programs(0) - 1)
    def _():
        second = jnp.concatenate([second_mine_ref[...], second_other_ref[...]], axis=0)
        at = lax.broadcasted_iota(jnp.int32, (nblk, second.shape[1]), 1)
        pick = jnp.where(at == pick_ref[...], 1.0, 0.0).astype(BF)
        contrib = dot(pick, second, NT) * fold[...]
        at = lax.broadcasted_iota(jnp.int32, (out_ref.shape[0], nblk), 0)
        place = jnp.where(at == owner_ref[...], 1.0, 0.0).astype(BF)
        high = contrib.astype(BF)
        rest = contrib - high.astype(F32)
        middle = rest.astype(BF)
        low = (rest - middle.astype(F32)).astype(BF)
        out_ref[...] = dot(place, high, NN) + (dot(place, middle, NN) + dot(place, low, NN))


def fold_rows(highs, lows, cuts, mine, other, second_mine, second_other, pick, owner, slab):
    n_hi, _, lo = highs[0].shape
    nblk = cuts[-1][1]
    half = mine.shape[0]
    rank = 2 * half
    per = min(n_hi, 4)
    spread_specs = [pl.BlockSpec((per, stop - start, lo), lambda g: (g, 0, 0)) for start, stop in cuts]
    return pl.pallas_call(
        functools.partial(fold_kernel, per, cuts),
        grid=(n_hi // per,),
        in_specs=spread_specs * 2
        + [pl.BlockSpec((half, per * lo), lambda g: (0, g))] * 2
        + [pl.BlockSpec(second_mine.shape, lambda g: (0, 0))] * 2
        + [
            pl.BlockSpec((nblk, 1), lambda g: (0, 0)),
            pl.BlockSpec((1, nblk), lambda g: (0, 0)),
        ],
        out_specs=[pl.BlockSpec((slab, rank), lambda g: (0, 0)), pl.BlockSpec((rank, rank), lambda g: (0, 0))],
        out_shape=[jax.ShapeDtypeStruct((slab, rank), F32), jax.ShapeDtypeStruct((rank, rank), F32)],
        scratch_shapes=[pltpu.VMEM((nblk, rank), F32)],
        compiler_params=pltpu.CompilerParams(vmem_limit_bytes=50 * 1024 * 1024),
        cost_estimate=pl.CostEstimate(flops=10_000_000_000, bytes_accessed=4 * n_hi * nblk * lo, transcendentals=0),
        name="fold_rows",
    )(*highs, *lows, mine, other, second_mine, second_other, pick, owner)


def small_inverse(block):
    n = block.shape[0]
    down = lax.broadcasted_iota(jnp.int32, (n, n), 0)
    across = lax.broadcasted_iota(jnp.int32, (n, n), 1)
    for j in range(n):
        column = block[:, j : j + 1]
        pivot = 1.0 / block[j : j + 1, j : j + 1]
        cleared = jnp.where(across == j, jnp.where(down == j, 1.0, 0.0), block)
        row = cleared[j : j + 1, :] * pivot
        block = jnp.where(down == j, row, cleared - column * row)
    return block


def invert_kernel(size, scale, left_ref, right_ref, out_ref):
    rank = left_ref.shape[1]
    exact = lax.Precision.HIGHEST
    a = (left_ref[...] / scale[0]) * (right_ref[...] / scale[1])
    down = lax.broadcasted_iota(jnp.int32, (rank, size), 0)
    eye = jnp.where(
        lax.broadcasted_iota(jnp.int32, (size, size), 0) == lax.broadcasted_iota(jnp.int32, (size, size), 1), 1.0, 0.0
    )
    for k in range(rank // size):
        s, e = k * size, (k + 1) * size
        inverse = small_inverse(a[s:e, s:e])
        column = jnp.where((down >= s) & (down < e), 0.0, a[:, s:e])
        pieces = [a[s:e, :s]] * (s > 0) + [eye] + [a[s:e, e:]] * (e < rank)
        row = dot(inverse, jnp.concatenate(pieces, axis=1), NN, exact)
        zero = jnp.zeros((rank, size), F32)
        pieces = [a[:, :s]] * (s > 0) + [zero] + [a[:, e:]] * (e < rank)
        a = jnp.concatenate(pieces, axis=1) - dot(column, row, NN, exact)
        pieces = [a[:s]] * (s > 0) + [row] + [a[e:]] * (e < rank)
        a = jnp.concatenate(pieces, axis=0)
    out_ref[...] = a


def invert(left, right, scale):
    rank = left.shape[1]
    return pl.pallas_call(
        functools.partial(invert_kernel, 32, scale),
        out_shape=jax.ShapeDtypeStruct((rank, rank), F32),
        cost_estimate=pl.CostEstimate(flops=10_000_000_000, bytes_accessed=1_000_000, transcendentals=0),
        name="invert",
    )(left, right)


def per_device(
    block_values,
    block_length,
    block_owner,
    block_second,
    block_third,
    live_blocks,
    second_factor,
    third_factor,
):
    n_rows = lax.axis_size("rows")
    n_cols = lax.axis_size("cols")
    row_at = lax.axis_index("rows")
    col_at = lax.axis_index("cols")
    nblk = block_values.shape[0]
    range_rows = second_factor.shape[0]
    third_rows = third_factor.shape[0]
    whole_third = third_rows * n_cols
    slab = range_rows * n_cols // n_rows
    n_hi = whole_third // LO
    mesh_axes = ("rows", "cols")

    def fetch(x, flip, shift):
        if flip == 0 and shift == 0:
            return x
        perm = [
            (r * n_cols + (c + shift) % n_cols, (r ^ flip) * n_cols + c) for r in range(n_rows) for c in range(n_cols)
        ]
        return lax.ppermute(x, mesh_axes, perm)

    second_t = second_factor.T
    third_t = third_factor.T
    both_t = jnp.concatenate([third_t, second_t], axis=1)
    mine = []
    for flip in range(0, n_rows, 2):
        first = fetch(both_t, flip, 0)
        others = [fetch(third_t, flip, shift) for shift in range(1, n_cols)]
        mine.append(jnp.concatenate([first[:, :third_rows]] + others + [first[:, third_rows:]], axis=1))
    mine = jnp.concatenate(mine, axis=0)
    other = fetch(mine, 1, 0)

    split = nblk * 3 // 4
    cuts = ((0, split), (split, nblk))
    turn = (col_at * third_rows).reshape(1)
    parts = [spread(live_blocks, turn, block_values, block_length[:, None], block_third, n_hi, *cut) for cut in cuts]

    second_mine, second_other = mine[:, whole_third:], other[:, whole_third:]
    second_range = jnp.concatenate([second_mine, second_other], axis=0)
    local = dot(second_range, second_range, NT)
    gram_second = local
    for shift in range(1, n_cols):
        gram_second = gram_second + fetch(local, 0, shift)
    partial_rows, gram_third = fold_rows(
        [part[0] for part in parts],
        [part[1] for part in parts],
        cuts,
        mine,
        other,
        second_mine,
        second_other,
        (block_second - col_at * range_rows)[:, None],
        (block_owner - row_at * slab)[None, :],
        slab,
    )
    owned_rows = slab // n_cols

    def chunk(shift):
        at = lax.rem(col_at - shift + n_cols, n_cols) * owned_rows
        return fetch(lax.dynamic_slice_in_dim(partial_rows, at, owned_rows, 0), 0, shift)

    total = chunk(0)
    for shift in range(1, n_cols):
        total = total + chunk(shift)
    inverse = invert(gram_second, gram_third, (range_rows * n_cols, whole_third))
    solved_t = dot(inverse, total, NT, lax.Precision.HIGHEST)

    share = n_rows // n_cols
    width = solved_t.shape[0] // n_rows
    offset = lax.rem(row_at, share) * n_cols + col_at
    tiles = []
    for step in range(n_rows):
        perm = [
            (r * n_cols + c, ((r % share) * n_cols + c + step) % n_rows * n_cols + r // share)
            for r in range(n_rows)
            for c in range(n_cols)
        ]
        place = jnp.bitwise_xor(lax.rem(offset + step, n_rows), row_at)
        place = (place & 1) * (n_rows // 2) + place // 2
        tiles.append(lax.ppermute(lax.dynamic_slice_in_dim(solved_t, place * width, width, 0), mesh_axes, perm))
    ordered = [tiles[-i % n_rows] for i in range(n_rows)]
    rolled = lax.dynamic_slice_in_dim(jnp.stack(ordered + ordered), lax.rem(n_rows - row_at, n_rows), n_rows, 0)
    return rolled.transpose(0, 2, 1).reshape(n_rows * owned_rows, width)


def solution(mesh):
    return jax.shard_map(
        per_device,
        mesh=mesh,
        in_specs=(
            P(("rows", "cols"), None),
            P(("rows", "cols")),
            P(("rows", "cols")),
            P(("rows", "cols")),
            P(("rows", "cols"), None),
            P(("rows", "cols")),
            P("cols", "rows"),
            P("cols", "rows"),
        ),
        out_specs=P("cols", "rows"),
        check_vma=False,
    )
```

```python
import functools

import jax
import jax.numpy as jnp
from jax import lax
from jax.experimental import pallas as pl
from jax.experimental.pallas import tpu as pltpu
from jax.sharding import PartitionSpec as P

LO = 256
BF = jnp.bfloat16
F32 = jnp.float32
NT = (((1,), (1,)), ((), ()))
NN = (((1,), (0,)), ((), ()))
TN = (((0,), (0,)), ((), ()))


def dot(a, b, dims, precision=None):
    return lax.dot_general(a, b, dims, precision=precision, preferred_element_type=F32)


def gather_steps(n_cols, n_rows, steps, both_ref, mine_ref, other_ref, sems):
    send, land, hand, take, own = sems
    rank, span = both_ref.shape
    row_at, col_at = lax.axis_index("rows"), lax.axis_index("cols")
    step = pl.program_id(0)
    pieces = [(flip, shift) for flip in range(0, n_rows, 2) for shift in range(n_cols)]
    partner = row_at + 1 - 2 * lax.rem(row_at, 2)

    def flipped(flip):
        target = row_at
        bit = 1
        while bit < n_rows:
            if flip & bit:
                target = target + bit - 2 * bit * lax.rem(row_at // bit, 2)
            bit *= 2
        return target

    def area(ref, i):
        flip, shift = pieces[i]
        return ref.at[pl.ds(flip // 2 * rank, rank), pl.ds(shift * span, span)]

    def out_copy(i):
        flip, shift = pieces[i]
        target = lax.rem(col_at - shift + n_cols, n_cols)
        return pltpu.make_async_remote_copy(
            src_ref=both_ref,
            dst_ref=area(mine_ref, i),
            send_sem=send.at[i],
            recv_sem=land.at[i],
            device_id=(flipped(flip), target),
            device_id_type=pl.DeviceIdType.MESH,
        )

    def core_copy(i):
        return pltpu.make_async_remote_copy(
            src_ref=both_ref if i == 0 else area(mine_ref, i),
            dst_ref=area(other_ref, i),
            send_sem=hand.at[i],
            recv_sem=take.at[i],
            device_id=(partner, col_at),
            device_id_type=pl.DeviceIdType.MESH,
        )

    def begin():
        barrier = pltpu.get_barrier_semaphore()
        pl.semaphore_signal(barrier, inc=1, device_id=(partner, col_at), device_id_type=pl.DeviceIdType.MESH)
        for flip, shift in pieces[1:]:
            pl.semaphore_signal(
                barrier,
                inc=1,
                device_id=(flipped(flip), lax.rem(col_at - shift + n_cols, n_cols)),
                device_id_type=pl.DeviceIdType.MESH,
            )
        pl.semaphore_wait(barrier, len(pieces))
        for i in range(1, len(pieces)):
            out_copy(i).start()
        core_copy(0).start()
        pltpu.make_async_copy(both_ref, area(mine_ref, 0), own).start()

    def relay(which):
        for i in which:
            out_copy(i).wait_recv()
            core_copy(i).start()

    def end():
        pltpu.make_async_copy(both_ref, area(mine_ref, 0), own).wait()
        for i in range(1, len(pieces)):
            out_copy(i).wait_send()
        for i in range(len(pieces)):
            core_copy(i).wait()

    late = steps // 2
    waves = steps - late
    rest = list(range(1, len(pieces)))
    size = -(-len(rest) // waves)
    pl.when(step == 0)(begin)
    for wave in range(waves):
        pl.when(step == late + wave)(functools.partial(relay, rest[wave * size : (wave + 1) * size]))
    return functools.partial(pl.when(step == steps - 1), end)


def spread_kernel(
    group,
    n_hi,
    n_cols,
    n_rows,
    steps,
    count_ref,
    turn_ref,
    values_ref,
    length_ref,
    third_ref,
    both_ref,
    high_ref,
    low_ref,
    mine_ref,
    other_ref,
    masked,
    rows,
    *sems,
):
    finish = gather_steps(n_cols, n_rows, steps, both_ref, mine_ref, other_ref, sems)
    width = values_ref.shape[1]
    base = pl.program_id(0) * group
    turn = turn_ref[0]
    lane = lax.broadcasted_iota(jnp.int32, (group, width), 1)
    slot = lax.broadcasted_iota(jnp.int32, (group, width), 0) + base
    live = (lane < length_ref[...]) & (slot < count_ref[0])
    masked[...] = jnp.where(live, values_ref[...].astype(F32), 0.0)
    at_hi = lax.broadcasted_iota(jnp.int32, (n_hi, width), 0)
    at_lo = lax.broadcasted_iota(jnp.int32, (LO, width), 0)

    def eight(step, carry):
        first = pl.multiple_of(step * 8, 8)
        index = third_ref[pl.ds(first, 8), :] - turn
        index = jnp.where(index < 0, index + n_hi * LO, index)
        value = masked[pl.ds(first, 8), :]
        index_hi = index // LO
        index_lo = index - index_hi * LO
        for j in range(8):
            left = jnp.where(at_hi == index_hi[j : j + 1, :], value[j : j + 1, :], 0.0).astype(BF)
            right = jnp.where(at_lo == index_lo[j : j + 1, :], 1.0, 0.0).astype(BF)
            dense = dot(left, right, NT)
            start = pl.multiple_of((first + j) * n_hi, n_hi)
            for piece in range(LO // 128):
                rows[piece, pl.ds(start, n_hi), :] = dense[:, piece * 128 : (piece + 1) * 128]
        return carry

    lax.fori_loop(0, group // 8, eight, 0)
    for h in range(n_hi):
        for piece in range(LO // 128):
            part = rows[piece, pl.ds(h, group, stride=n_hi), :]
            high = part.astype(BF)
            high_ref[h, :, piece * 128 : (piece + 1) * 128] = high
            low_ref[h, :, piece * 128 : (piece + 1) * 128] = (part - high.astype(F32)).astype(BF)
    finish()


def spread(count, turn, values, length, third, both, n_hi, n_cols, n_rows):
    nblk, width = values.shape
    group = min(nblk, 64 if n_hi <= 64 else 32)
    steps = nblk // group
    rank, span = both.shape
    n_pieces = n_rows // 2 * n_cols
    gathered = jax.ShapeDtypeStruct((rank * (n_rows // 2), span * n_cols), BF)
    return pl.pallas_call(
        functools.partial(spread_kernel, group, n_hi, n_cols, n_rows, steps),
        grid=(steps,),
        in_specs=[
            pl.BlockSpec(memory_space=pltpu.SMEM),
            pl.BlockSpec(memory_space=pltpu.SMEM),
            pl.BlockSpec((group, width), lambda g: (g, 0)),
            pl.BlockSpec((group, 1), lambda g: (g, 0)),
            pl.BlockSpec((group, width), lambda g: (g, 0)),
            pl.BlockSpec(memory_space=pl.ANY),
        ],
        out_specs=[pl.BlockSpec((n_hi, group, LO), lambda g: (0, g, 0))] * 2 + [pl.BlockSpec(memory_space=pl.ANY)] * 2,
        out_shape=[jax.ShapeDtypeStruct((n_hi, nblk, LO), BF)] * 2 + [gathered] * 2,
        scratch_shapes=[pltpu.VMEM((group, width), F32), pltpu.VMEM((LO // 128, group * n_hi, 128), F32)]
        + [pltpu.SemaphoreType.DMA((n_pieces,))] * 4
        + [pltpu.SemaphoreType.DMA],
        compiler_params=pltpu.CompilerParams(
            vmem_limit_bytes=32 * 1024 * 1024, collective_id=0, has_side_effects=True
        ),
        name="gather_spread",
    )(count, turn, values, length, third, both)


def exchange_kernel(n_rows, n_cols, tiles_ref, out_ref, send, land, own):
    row_at, col_at = lax.axis_index("rows"), lax.axis_index("cols")
    share = n_rows // n_cols
    offset = lax.rem(row_at, share) * n_cols + col_at
    home = row_at // share
    barrier = pltpu.get_barrier_semaphore()
    for r in range(n_rows):
        for c in range(n_cols):

            @pl.when((row_at != r) | (col_at != c))
            def _():
                pl.semaphore_signal(barrier, inc=1, device_id=(r, c), device_id_type=pl.DeviceIdType.MESH)

    pl.semaphore_wait(barrier, n_rows * n_cols - 1)

    def copy(step):
        target = lax.rem(offset + step, n_rows)
        remote = pltpu.make_async_remote_copy(
            src_ref=tiles_ref.at[step],
            dst_ref=out_ref.at[step],
            send_sem=send.at[step],
            recv_sem=land.at[step],
            device_id=(target, home),
            device_id_type=pl.DeviceIdType.MESH,
        )
        return (target == row_at) & (home == col_at), remote, pltpu.make_async_copy(tiles_ref.at[step], out_ref.at[step], own)

    for step in range(n_rows):
        stays, remote, local = copy(step)
        pl.when(jnp.logical_not(stays))(remote.start)
        pl.when(stays)(local.start)
    for step in range(n_rows):
        stays, remote, local = copy(step)
        pl.when(jnp.logical_not(stays))(remote.wait)
        pl.when(stays)(local.wait)


def exchange(tiles, n_rows, n_cols):
    return pl.pallas_call(
        functools.partial(exchange_kernel, n_rows, n_cols),
        in_specs=[pl.BlockSpec(memory_space=pltpu.VMEM)],
        out_specs=pl.BlockSpec(memory_space=pltpu.VMEM),
        out_shape=jax.ShapeDtypeStruct(tiles.shape, F32),
        scratch_shapes=[
            pltpu.SemaphoreType.DMA((n_rows,)),
            pltpu.SemaphoreType.DMA((n_rows,)),
            pltpu.SemaphoreType.DMA,
        ],
        compiler_params=pltpu.CompilerParams(collective_id=1, has_side_effects=True),
        name="exchange",
    )(tiles)


def fold_kernel(per, *refs):
    high_ref, low_ref, mine_ref, other_ref, second_mine_ref, second_other_ref, strip_mine_ref, strip_other_ref = refs[:8]
    pick_ref, owner_ref, out_ref, gram_second_ref, gram_ref, fold = refs[8:]
    step = pl.program_id(0)
    nblk = fold.shape[0]

    @pl.when(step == 0)
    def _():
        fold[...] = jnp.zeros_like(fold)
        gram_ref[...] = jnp.zeros_like(gram_ref)
        gram_second_ref[...] = jnp.zeros_like(gram_second_ref)

    table = jnp.concatenate([mine_ref[...], other_ref[...]], axis=0)
    gram_ref[...] += dot(table, table, NT)
    strip = jnp.concatenate([strip_mine_ref[...], strip_other_ref[...]], axis=0)
    gram_second_ref[...] += dot(strip, strip, NT)
    total = fold[...]
    for h in range(per):
        piece = table[:, h * LO : (h + 1) * LO]
        total = total + (dot(high_ref[h], piece, NT) + dot(low_ref[h], piece, NT))
    fold[...] = total

    @pl.when(step == pl.num_programs(0) - 1)
    def _():
        second = jnp.concatenate([second_mine_ref[...], second_other_ref[...]], axis=0)
        at = lax.broadcasted_iota(jnp.int32, (nblk, second.shape[1]), 1)
        pick = jnp.where(at == pick_ref[...], 1.0, 0.0).astype(BF)
        contrib = dot(pick, second, NT) * fold[...]
        at = lax.broadcasted_iota(jnp.int32, (out_ref.shape[0], nblk), 0)
        place = jnp.where(at == owner_ref[...], 1.0, 0.0).astype(BF)
        high = contrib.astype(BF)
        rest = contrib - high.astype(F32)
        middle = rest.astype(BF)
        low = (rest - middle.astype(F32)).astype(BF)
        out_ref[...] = dot(place, high, NN) + (dot(place, middle, NN) + dot(place, low, NN))


def fold_rows(high, low, mine, other, pick, owner, slab, third_rows, range_rows):
    n_hi, nblk, lo = high.shape
    half = mine.shape[0]
    rank = 2 * half
    per = 4
    steps = n_hi // per
    unit = per * lo
    n_cols = n_hi * lo // third_rows
    span = third_rows + range_rows
    strip = n_cols * range_rows // steps
    wide, narrow = third_rows // unit, range_rows // strip
    assert third_rows % unit == 0 and span % unit == 0 and third_rows % range_rows == 0
    assert range_rows % strip == 0 and third_rows % strip == 0
    return pl.pallas_call(
        functools.partial(fold_kernel, per),
        grid=(steps,),
        in_specs=[pl.BlockSpec((per, nblk, lo), lambda g: (g, 0, 0))] * 2
        + [pl.BlockSpec((half, unit), lambda g: (0, g // wide * (span // unit) + g % wide))] * 2
        + [pl.BlockSpec((half, range_rows), lambda g: (0, third_rows // range_rows))] * 2
        + [
            pl.BlockSpec((half, strip), lambda g: (0, g // narrow * (span // strip) + third_rows // strip + g % narrow))
        ]
        * 2
        + [
            pl.BlockSpec((nblk, 1), lambda g: (0, 0)),
            pl.BlockSpec((1, nblk), lambda g: (0, 0)),
        ],
        out_specs=[pl.BlockSpec((slab, rank), lambda g: (0, 0))] + [pl.BlockSpec((rank, rank), lambda g: (0, 0))] * 2,
        out_shape=[jax.ShapeDtypeStruct((slab, rank), F32)] + [jax.ShapeDtypeStruct((rank, rank), F32)] * 2,
        scratch_shapes=[pltpu.VMEM((nblk, rank), F32)],
        compiler_params=pltpu.CompilerParams(vmem_limit_bytes=24 * 1024 * 1024),
        cost_estimate=pl.CostEstimate(flops=10_000_000_000, bytes_accessed=4 * n_hi * nblk * lo, transcendentals=0),
        name="fold_rows",
    )(high, low, mine, other, mine, other, mine, other, pick, owner)


def small_inverse(block):
    n = block.shape[0]
    down = lax.broadcasted_iota(jnp.int32, (n, n), 0)
    across = lax.broadcasted_iota(jnp.int32, (n, n), 1)
    for j in range(n):
        column = block[:, j : j + 1]
        pivot = 1.0 / block[j : j + 1, j : j + 1]
        cleared = jnp.where(across == j, jnp.where(down == j, 1.0, 0.0), block)
        row = cleared[j : j + 1, :] * pivot
        block = jnp.where(down == j, row, cleared - column * row)
    return block


def invert_kernel(size, scale, left_ref, right_ref, out_ref):
    rank = left_ref.shape[1]
    exact = lax.Precision.HIGHEST
    a = (left_ref[...] / scale[0]) * (right_ref[...] / scale[1])
    down = lax.broadcasted_iota(jnp.int32, (rank, size), 0)
    eye = jnp.where(
        lax.broadcasted_iota(jnp.int32, (size, size), 0) == lax.broadcasted_iota(jnp.int32, (size, size), 1), 1.0, 0.0
    )
    for k in range(rank // size):
        s, e = k * size, (k + 1) * size
        inverse = small_inverse(a[s:e, s:e])
        column = jnp.where((down >= s) & (down < e), 0.0, a[:, s:e])
        pieces = [a[s:e, :s]] * (s > 0) + [eye] + [a[s:e, e:]] * (e < rank)
        row = dot(inverse, jnp.concatenate(pieces, axis=1), NN, exact)
        zero = jnp.zeros((rank, size), F32)
        pieces = [a[:, :s]] * (s > 0) + [zero] + [a[:, e:]] * (e < rank)
        a = jnp.concatenate(pieces, axis=1) - dot(column, row, NN, exact)
        pieces = [a[:s]] * (s > 0) + [row] + [a[e:]] * (e < rank)
        a = jnp.concatenate(pieces, axis=0)
    out_ref[...] = a


def invert(left, right, scale):
    rank = left.shape[1]
    return pl.pallas_call(
        functools.partial(invert_kernel, 32, scale),
        out_shape=jax.ShapeDtypeStruct((rank, rank), F32),
        cost_estimate=pl.CostEstimate(flops=10_000_000_000, bytes_accessed=1_000_000, transcendentals=0),
        name="invert",
    )(left, right)


def per_device(
    block_values,
    block_length,
    block_owner,
    block_second,
    block_third,
    live_blocks,
    second_factor,
    third_factor,
):
    n_rows = lax.axis_size("rows")
    n_cols = lax.axis_size("cols")
    row_at = lax.axis_index("rows")
    col_at = lax.axis_index("cols")
    nblk = block_values.shape[0]
    range_rows = second_factor.shape[0]
    third_rows = third_factor.shape[0]
    whole_third = third_rows * n_cols
    slab = range_rows * n_cols // n_rows
    n_hi = whole_third // LO
    mesh_axes = ("rows", "cols")

    def fetch(x, flip, shift):
        if flip == 0 and shift == 0:
            return x
        perm = [
            (r * n_cols + (c + shift) % n_cols, (r ^ flip) * n_cols + c) for r in range(n_rows) for c in range(n_cols)
        ]
        return lax.ppermute(x, mesh_axes, perm)

    both_t = jnp.concatenate([third_factor.T, second_factor.T], axis=1)
    turn = (col_at * third_rows).reshape(1)
    high, low, mine, other = spread(
        live_blocks, turn, block_values, block_length[:, None], block_third, both_t, n_hi, n_cols, n_rows
    )
    partial_rows, gram_second, gram_third = fold_rows(
        high,
        low,
        mine,
        other,
        (block_second - col_at * range_rows)[:, None],
        (block_owner - row_at * slab)[None, :],
        slab,
        third_rows,
        range_rows,
    )
    owned_rows = slab // n_cols

    def chunk(shift):
        at = lax.rem(col_at - shift + n_cols, n_cols) * owned_rows
        return fetch(lax.dynamic_slice_in_dim(partial_rows, at, owned_rows, 0), 0, shift)

    total = chunk(0)
    for shift in range(1, n_cols):
        total = total + chunk(shift)
    inverse = invert(gram_second, gram_third, (range_rows * n_cols, whole_third))
    solved_t = dot(inverse, total, NT, lax.Precision.HIGHEST)

    share = n_rows // n_cols
    width = solved_t.shape[0] // n_rows
    offset = lax.rem(row_at, share) * n_cols + col_at
    tiles = []
    for step in range(n_rows):
        place = jnp.bitwise_xor(lax.rem(offset + step, n_rows), row_at)
        place = (place & 1) * (n_rows // 2) + place // 2
        tiles.append(lax.dynamic_slice_in_dim(solved_t, place * width, width, 0))
    moved = exchange(jnp.stack(tiles), n_rows, n_cols)
    ordered = [moved[-i % n_rows] for i in range(n_rows)]
    rolled = lax.dynamic_slice_in_dim(jnp.stack(ordered + ordered), lax.rem(n_rows - row_at, n_rows), n_rows, 0)
    return rolled.transpose(0, 2, 1).reshape(n_rows * owned_rows, width)


def solution(mesh):
    return jax.shard_map(
        per_device,
        mesh=mesh,
        in_specs=(
            P(("rows", "cols"), None),
            P(("rows", "cols")),
            P(("rows", "cols")),
            P(("rows", "cols")),
            P(("rows", "cols"), None),
            P(("rows", "cols")),
            P("cols", "rows"),
            P("cols", "rows"),
        ),
        out_specs=P("cols", "rows"),
        check_vma=False,
    )
```
